32 devices in a mesh: head: 2 (over y), ctx: 4 (over z), batch: 4 (over x, core).
Axes of the slice: x: 2, y: 2, z: 4, core: 2. Of those that a mesh axis runs over, the one named last changes fastest.
Arguments:
- tokens: bfloat16 [4, 1024, 1024], P('batch', ('ctx', 'head')), may hold values from -6 to 6
- cotangent: bfloat16 [4, 1024, 1024], P('batch', ('ctx', 'head')), may hold values from -6 to 6
- norm1_gain: bfloat16 [1024], P(('head', 'ctx', 'batch')), may hold values from 0.5 to 1.5
- w_query: bfloat16 [1024, 1024], P(('head', 'ctx', 'batch')), may hold values from -0.1875 to 0.1875
- w_key: bfloat16 [1024, 1024], P(('head', 'ctx', 'batch')), may hold values from -0.1875 to 0.1875
- w_value: bfloat16 [1024, 2048], P(('head', 'ctx', 'batch')), may hold values from -0.1875 to 0.1875
- w_gate: bfloat16 [1024, 2048], P(('head', 'ctx', 'batch')), may hold values from -0.1875 to 0.1875
- w_rates: bfloat16 [1024, 16], P(('head', 'ctx', 'batch')), may hold values from -0.1875 to 0.1875
- conv_query: bfloat16 [4, 1024], P(None, 'head'), may hold values from -3 to 3
- conv_key: bfloat16 [4, 1024], P(None, 'head'), may hold values from -3 to 3
- conv_value: bfloat16 [4, 2048], P(None, 'head'), may hold values from -3 to 3
- decay_log: float32 [8], P('head'), may hold values from -7 to 0.5
- decay_bias: float32 [8], P('head'), may hold values from -4 to 1
- out_gain: bfloat16 [2048], P('head'), may hold values from 0.5 to 1.5
- w_out: bfloat16 [1024, 2048], P(('head', 'ctx', 'batch')), may hold values from -0.125 to 0.125
- norm2_gain: bfloat16 [1024], P(('head', 'ctx', 'batch')), may hold values from 0.5 to 1.5
- w_ffgate: bfloat16 [1024, 2816], P(('head', 'ctx', 'batch')), may hold values from -0.1875 to 0.1875
- w_ffup: bfloat16 [1024, 2816], P(('head', 'ctx', 'batch')), may hold values from -0.1875 to 0.1875
- w_down: bfloat16 [1024, 2816], P(('head', 'ctx', 'batch')), may hold values from -0.109375 to 0.109375
Outputs:
- output: bfloat16 [4, 1024, 1024], P('batch', ('ctx', 'head'))
- input_grad: float32 [4, 1024, 1024], P('batch', ('ctx', 'head'))
- g_norm1: float32 [1024], P(('head', 'ctx', 'batch'))
- g_query: float32 [1024, 1024], P(('ctx', 'batch'), 'head')
- g_key: float32 [1024, 1024], P(('ctx', 'batch'), 'head')
- g_value: float32 [1024, 2048], P(('ctx', 'batch'), 'head')
- g_gate: float32 [1024, 2048], P(('ctx', 'batch'), 'head')
- g_rates: float32 [1024, 16], P(('ctx', 'batch'), 'head')
- g_conv_query: float32 [4, 1024], P(None, 'head')
- g_conv_key: float32 [4, 1024], P(None, 'head')
- g_conv_value: float32 [4, 2048], P(None, 'head')
- g_decay_log: float32 [8], P('head')
- g_decay_bias: float32 [8], P('head')
- g_out_gain: float32 [2048], P('head')
- g_out: float32 [1024, 2048], P(('ctx', 'batch'), 'head')
- g_norm2: float32 [1024], P(('head', 'ctx', 'batch'))
- g_ffgate: float32 [1024, 2816], P(('ctx', 'batch'), 'head')
- g_ffup: float32 [1024, 2816], P(('ctx', 'batch'), 'head')
- g_down: float32 [1024, 2816], P(('ctx', 'batch'), 'head')
The draws below stay inside these ranges and needn't reach their ends.
All inputs are finite; a program needn't handle non-finite values.
Results may differ from the reference program's by a relative error of at most 0.02.
Values may be sent and summed in bfloat16 or wider, within the bound.
A program may use at most 256 MiB of HBM per device.

```python
import math
import jax
import jax.numpy as jnp
from jax import lax

D = 1024
H = 8
DK = 128
DV = 256
FF = 2816
KW = 4
SPAN = 64
SEQS = 4
PIECE = 256
LENGTH = 1024
N_CTX = 4


def block_levels(rng, shape, pieces, least, largest):
    level = 1.0
    for axis_at, parts in pieces:
        draws = jax.random.uniform(jax.random.fold_in(jax.random.fold_in(rng, 6), axis_at), (parts,), jnp.float32, least / len(pieces), largest / len(pieces))
        level = level * jnp.repeat(jnp.exp(draws), shape[axis_at] // parts).reshape((-1,) + (1,) * (len(shape) - 1 - axis_at))
    return level


def gaussian(stream_key, extent, scale, bound, cuts=(), kind=jnp.bfloat16):
    drawn = jax.random.normal(stream_key, extent, jnp.float32) * scale
    if len(cuts) > 0:
        drawn = block_levels(stream_key, extent, cuts, -0.22, 0.18) * drawn
    return jnp.clip(drawn, min=-bound, max=bound).astype(kind)


def setup_inputs(seed: int = 0) -> dict:
    key_list = jax.random.split(jax.random.key(seed), 20)
    tokens = gaussian(key_list[0], (SEQS, LENGTH, D), 1.0, 6.0, ((0, 4), (1, 8)))
    cotangent = gaussian(key_list[1], (SEQS, LENGTH, D), 1.0, 6.0, ((0, 4), (1, 8)))
    norm1_gain = jnp.clip(1.0 + 0.1 * jax.random.normal(key_list[2], (D,), jnp.float32), 0.5, 1.5).astype(jnp.bfloat16)
    w_query = gaussian(key_list[3], (D, H * DK), D ** -0.5, 0.1875, ((0, 32),))
    w_key = gaussian(key_list[4], (D, H * DK), D ** -0.5, 0.1875, ((0, 32),))
    w_value = gaussian(key_list[5], (D, H * DV), D ** -0.5, 0.1875, ((0, 32),))
    w_gate = gaussian(key_list[6], (D, H * DV), D ** -0.5, 0.1875, ((0, 32),))
    w_rates = gaussian(key_list[7], (D, 2 * H), D ** -0.5, 0.1875, ((0, 32),))
    conv_query = gaussian(key_list[8], (KW, H * DK), KW ** -0.5, 3.0, ((1, 2),))
    conv_key = gaussian(key_list[9], (KW, H * DK), KW ** -0.5, 3.0, ((1, 2),))
    conv_value = gaussian(key_list[10], (KW, H * DV), KW ** -0.5, 3.0, ((1, 2),))
    decay_log = jnp.clip(-7.0 + 7.5 * jax.random.uniform(key_list[11], (H,), jnp.float32) ** block_levels(key_list[11], (H,), ((0, 2),), -0.2, 0.2), -7.0, 0.5)
    decay_bias = jnp.clip(-4.0 + 5.0 * jax.random.uniform(key_list[12], (H,), jnp.float32) ** block_levels(key_list[12], (H,), ((0, 2),), -0.2, 0.2), -4.0, 1.0)
    out_gain = jnp.clip(1.0 + 0.1 * jax.random.normal(key_list[13], (H * DV,), jnp.float32), 0.5, 1.5).astype(jnp.bfloat16)
    w_out = gaussian(key_list[14], (D, H * DV), (H * DV) ** -0.5, 0.125, ((0, 32),))
    norm2_gain = jnp.clip(1.0 + 0.1 * jax.random.normal(key_list[15], (D,), jnp.float32), 0.5, 1.5).astype(jnp.bfloat16)
    w_ffgate = gaussian(key_list[16], (D, FF), D ** -0.5, 0.1875, ((0, 32),))
    w_ffup = gaussian(key_list[17], (D, FF), D ** -0.5, 0.1875, ((0, 32),))
    w_down = gaussian(key_list[18], (D, FF), FF ** -0.5, 0.109375, ((0, 32),))
    return {"tokens": tokens, "cotangent": cotangent, "norm1_gain": norm1_gain, "w_query": w_query, "w_key": w_key, "w_value": w_value, "w_gate": w_gate, "w_rates": w_rates, "conv_query": conv_query, "conv_key": conv_key, "conv_value": conv_value, "decay_log": decay_log, "decay_bias": decay_bias, "out_gain": out_gain, "w_out": w_out, "norm2_gain": norm2_gain, "w_ffgate": w_ffgate, "w_ffup": w_ffup, "w_down": w_down}


epsilon = 1e-06
highest_precision = lax.Precision.HIGHEST

def mat_nt(first_mat, second_mat):
    return lax.dot_general(first_mat.astype(jnp.float32), second_mat.astype(jnp.float32), (((1,), (1,)), ((), ())), preferred_element_type=jnp.float32)

def mat_tn(first_mat, second_mat):
    return lax.dot_general(first_mat.astype(jnp.float32), second_mat.astype(jnp.float32), (((0,), (0,)), ((), ())), preferred_element_type=jnp.float32)

def piece_total(left_rows, right_rows):
    left_pieces = left_rows.reshape(N_CTX, PIECE, left_rows.shape[1])
    right_pieces = right_rows.reshape(N_CTX, PIECE, right_rows.shape[1])

    def add_piece(running, operands):
        rounded = lax.optimization_barrier(mat_tn(operands[0], operands[1]).astype(jnp.bfloat16))
        return (running + rounded.astype(jnp.float32), None)
    start_sum = jnp.zeros((left_rows.shape[1], right_rows.shape[1]), jnp.float32)
    running, unused_rows = lax.scan(add_piece, start_sum, (left_pieces, right_pieces))
    return running

def rms_scale(hidden, gain_vec):
    return hidden * lax.rsqrt(lax.optimization_barrier(jnp.mean(hidden * hidden, axis=-1, keepdims=True)) + epsilon) * gain_vec

def swiglu(gate_part, up_part):
    return jax.nn.silu(gate_part) * up_part

def unit_rows(matrix):
    return matrix * lax.rsqrt(lax.optimization_barrier(jnp.sum(matrix * matrix, axis=-1, keepdims=True)) + epsilon)

def prepare(padded, conv_all, rates, decay_log, decay_bias):
    head_count = decay_log.shape[0]
    length = padded.shape[0] - (KW - 1)
    mixed_rows = padded[0:length] * conv_all[0]
    for tap_index in range(1, KW):
        mixed_rows = mixed_rows + padded[tap_index:tap_index + length] * conv_all[tap_index]
    active = jax.nn.silu(mixed_rows)
    split_one = head_count * DK
    queries = unit_rows(active[:, :split_one].reshape(length, head_count, DK)) / math.sqrt(DK)
    keys_vec = unit_rows(active[:, split_one:2 * split_one].reshape(length, head_count, DK))
    values = active[:, 2 * split_one:].reshape(length, head_count, DV)
    rate_pairs = rates.reshape(length, head_count, 2)
    log_decay = -jnp.exp(decay_log) * jax.nn.softplus(rate_pairs[:, :, 0] + decay_bias)
    strength = jax.nn.sigmoid(rate_pairs[:, :, 1])
    return (queries, keys_vec, values, log_decay, strength)

def span_parts(keys_blk, values_blk, decay_blk, strength_blk):
    key_heads = jnp.transpose(keys_blk, (1, 0, 2))
    value_heads = jnp.transpose(values_blk, (1, 0, 2))
    cumulative = jnp.cumsum(jnp.transpose(decay_blk), axis=1)
    strength_heads = jnp.transpose(strength_blk)
    block_size = cumulative.shape[1]
    row_index = jnp.arange(block_size)[:, None]
    col_index = jnp.arange(block_size)[None, :]
    strict = row_index > col_index
    inclusive = row_index >= col_index
    gaps = cumulative[:, :, None] - cumulative[:, None, :]
    below_decay = jnp.where(strict, jnp.exp(jnp.where(strict, gaps, 0.0)), 0.0)
    key_gram = jnp.einsum('htd,hsd->hts', key_heads, key_heads, precision=highest_precision)
    system = jnp.eye(block_size, dtype=jnp.float32) + strength_heads[:, :, None] * below_decay * key_gram
    decay_factor = jnp.exp(cumulative)
    targets = jnp.concatenate([strength_heads[:, :, None] * value_heads, (strength_heads * decay_factor)[:, :, None] * key_heads], axis=2)
    solved = jax.scipy.linalg.solve_triangular(system, targets, lower=True, unit_diagonal=True)
    value_width = value_heads.shape[2]
    direct_term = solved[:, :, :value_width]
    across_devices_total = solved[:, :, value_width:]
    tail_decay = jnp.exp(cumulative[:, -1:] - cumulative)
    decayed_key_rows = tail_decay[:, :, None] * key_heads
    final_decay_factor = jnp.exp(cumulative[:, -1])
    within = jnp.where(inclusive, jnp.exp(jnp.where(inclusive, gaps, 0.0)), 0.0)
    return (key_heads, decay_factor, within, direct_term, across_devices_total, decayed_key_rows, final_decay_factor)

def delta_block(incoming_state, block_in):
    query_blk, keys_blk, values_blk, decay_blk, strength_blk = block_in
    key_heads, decay_factor, within, direct_term, across_devices_total, decayed_key_rows, final_decay_factor = span_parts(keys_blk, values_blk, decay_blk, strength_blk)
    query_head_rows = jnp.transpose(query_blk, (1, 0, 2))
    state_update = direct_term - jnp.einsum('nal,nlr->nar', across_devices_total, incoming_state, precision=highest_precision)
    scores = jnp.einsum('htd,hsd->hts', query_head_rows, key_heads, precision=highest_precision) * within
    layer_result = decay_factor[:, :, None] * jnp.einsum('nal,nlr->nar', query_head_rows, incoming_state, precision=highest_precision)
    layer_result = layer_result + jnp.einsum('hts,hsv->htv', scores, state_update, precision=highest_precision)
    updated_state = final_decay_factor[:, None, None] * incoming_state + jnp.einsum('pex,ped->pxd', decayed_key_rows, state_update, precision=highest_precision)
    return (updated_state, jnp.transpose(layer_result, (1, 0, 2)))

def into_blocks(tensor):
    return tensor.reshape((tensor.shape[0] // SPAN, SPAN) + tensor.shape[1:])

def mixer_out(queries, keys_vec, values, log_decay, strength, initial_state):
    final_state, outputs = lax.scan(delta_block, initial_state, (into_blocks(queries), into_blocks(keys_vec), into_blocks(values), into_blocks(log_decay), into_blocks(strength)))
    return outputs.reshape((queries.shape[0],) + outputs.shape[2:])

def out_gate(mixer_rows, gate_rows, gain_vec):
    normed = mixer_rows * lax.rsqrt(lax.optimization_barrier(jnp.mean(mixer_rows * mixer_rows, axis=-1, keepdims=True)) + epsilon)
    flat = normed.reshape(mixer_rows.shape[0], mixer_rows.shape[1] * mixer_rows.shape[2])
    return flat * gain_vec * jax.nn.silu(gate_rows)

def one_sequence(seq_tokens, seq_cot, params):
    norm1_gain, w_query, w_key, w_value, w_gate, w_rates, conv_query, conv_key, conv_value, decay_log, decay_bias, out_gain, w_out, norm2_gain, w_ffgate, w_ffup, w_down = params
    residual = seq_tokens.astype(jnp.float32)
    normed_f, norm_one_vjp = jax.vjp(rms_scale, residual, norm1_gain.astype(jnp.float32))
    normed_one = normed_f.astype(jnp.bfloat16)
    query_raw = jnp.dot(normed_one.astype(jnp.float32), w_query.astype(jnp.float32), preferred_element_type=jnp.float32).astype(jnp.bfloat16)
    key_raw = jnp.dot(normed_one.astype(jnp.float32), w_key.astype(jnp.float32), preferred_element_type=jnp.float32).astype(jnp.bfloat16)
    value_raw = jnp.dot(normed_one.astype(jnp.float32), w_value.astype(jnp.float32), preferred_element_type=jnp.float32).astype(jnp.bfloat16)
    gate_raw = jnp.dot(normed_one.astype(jnp.float32), w_gate.astype(jnp.float32), preferred_element_type=jnp.float32).astype(jnp.bfloat16)
    rates_raw = jnp.dot(normed_one.astype(jnp.float32), w_rates.astype(jnp.float32), preferred_element_type=jnp.float32).astype(jnp.bfloat16)
    joined = jnp.concatenate([query_raw, key_raw, value_raw], axis=1).astype(jnp.float32)
    padded = jnp.concatenate([jnp.zeros((KW - 1, joined.shape[1]), jnp.float32), joined], axis=0)
    conv_all = jnp.concatenate([conv_query, conv_key, conv_value], axis=1).astype(jnp.float32)
    prepared, prepare_vjp = jax.vjp(prepare, padded, conv_all, rates_raw.astype(jnp.float32), decay_log, decay_bias)
    queries, keys_vec, values, log_decay, strength = prepared
    zero_state = jnp.zeros((H, DK, DV), jnp.float32)
    mixer_rows, mixer_vjp = jax.vjp(mixer_out, queries, keys_vec, values, log_decay, strength, zero_state)
    gated_f, gate_vjp = jax.vjp(out_gate, mixer_rows, gate_raw.astype(jnp.float32), out_gain.astype(jnp.float32))
    gated = gated_f.astype(jnp.bfloat16)
    middle = residual + mat_nt(gated, w_out)
    normed_two_f, norm_two_vjp = jax.vjp(rms_scale, middle, norm2_gain.astype(jnp.float32))
    normed_two = normed_two_f.astype(jnp.bfloat16)
    ff_gate = jnp.dot(normed_two.astype(jnp.float32), w_ffgate.astype(jnp.float32), preferred_element_type=jnp.float32)
    ff_up = jnp.dot(normed_two.astype(jnp.float32), w_ffup.astype(jnp.float32), preferred_element_type=jnp.float32)
    hidden_f, swiglu_vjp = jax.vjp(swiglu, ff_gate, ff_up)
    hidden = hidden_f.astype(jnp.bfloat16)
    output_seq = (middle + mat_nt(hidden, w_down)).astype(jnp.bfloat16)
    hidden_grad = jnp.dot(seq_cot.astype(jnp.float32), w_down.astype(jnp.float32), preferred_element_type=jnp.float32)
    gate_grad_f, up_grad_f = swiglu_vjp(hidden_grad)
    ffgate_grad = gate_grad_f.astype(jnp.bfloat16)
    ffup_grad = up_grad_f.astype(jnp.bfloat16)
    normed_two_grad = mat_nt(ffgate_grad, w_ffgate) + mat_nt(ffup_grad, w_ffup)
    middle_part, gain_two_grad = norm_two_vjp(normed_two_grad)
    middle_grad = seq_cot.astype(jnp.float32) + middle_part
    middle_grad_b = middle_grad.astype(jnp.bfloat16)
    gated_grad = jnp.dot(middle_grad_b.astype(jnp.float32), w_out.astype(jnp.float32), preferred_element_type=jnp.float32).astype(jnp.bfloat16)
    mixer_grad, gate_grad_f2, out_gain_grad = gate_vjp(gated_grad.astype(jnp.float32))
    query_g, key_g, value_g, decay_g, strength_g, unused_state = mixer_vjp(mixer_grad)
    padded_grad, conv_grad, rates_grad_f, decay_log_grad, decay_bias_grad = prepare_vjp((query_g, key_g, value_g, decay_g, strength_g))
    raw_grad = padded_grad[KW - 1:].astype(jnp.bfloat16)
    query_width = H * DK
    query_grad = raw_grad[:, :query_width]
    key_grad = raw_grad[:, query_width:2 * query_width]
    value_grad = raw_grad[:, 2 * query_width:]
    gate_grad = gate_grad_f2.astype(jnp.bfloat16)
    rates_grad = rates_grad_f.astype(jnp.bfloat16)
    normed_one_grad = mat_nt(query_grad, w_query) + mat_nt(key_grad, w_key) + mat_nt(value_grad, w_value) + mat_nt(gate_grad, w_gate) + mat_nt(rates_grad, w_rates)
    input_part, gain_one_grad = norm_one_vjp(normed_one_grad)
    input_grad = middle_grad + input_part
    grads = (gain_one_grad, piece_total(normed_one, query_grad), piece_total(normed_one, key_grad), piece_total(normed_one, value_grad), piece_total(normed_one, gate_grad), piece_total(normed_one, rates_grad), conv_grad[:, :query_width], conv_grad[:, query_width:2 * query_width], conv_grad[:, 2 * query_width:], decay_log_grad, decay_bias_grad, out_gain_grad, piece_total(middle_grad_b, gated), gain_two_grad, piece_total(normed_two, ffgate_grad), piece_total(normed_two, ffup_grad), piece_total(seq_cot, hidden))
    return (output_seq, input_grad, grads)

def reference(tokens, cotangent, norm1_gain, w_query, w_key, w_value, w_gate, w_rates, conv_query, conv_key, conv_value, decay_log, decay_bias, out_gain, w_out, norm2_gain, w_ffgate, w_ffup, w_down):
    params = (norm1_gain, w_query, w_key, w_value, w_gate, w_rates, conv_query, conv_key, conv_value, decay_log, decay_bias, out_gain, w_out, norm2_gain, w_ffgate, w_ffup, w_down)
    totals_init = tuple((jnp.zeros(param.shape, jnp.float32) for param in params))

    def per_sequence(totals, pair):
        output_seq, input_grad, grads = one_sequence(pair[0], pair[1], params)
        return (jax.tree.map(jnp.add, totals, grads), (output_seq, input_grad))
    totals, stacked = lax.scan(per_sequence, totals_init, (tokens, cotangent))
    return (stacked[0], stacked[1], totals[0], totals[1], totals[2], totals[3], totals[4], totals[5], totals[6], totals[7], totals[8], totals[9], totals[10], totals[11], totals[12], totals[13], totals[14], totals[15], totals[16])
```

```python
import math

import jax
import jax.numpy as jnp
from jax import lax
from jax.experimental import pallas as pl
from jax.experimental.pallas import tpu as pltpu
from jax.sharding import PartitionSpec as P

KW = 4
CHUNK = 256
epsilon = 1e-06
highest_precision = lax.Precision.HIGHEST


def passed_along(block, axis, distance):
    devices = range(lax.axis_size(axis))
    route = [(i - distance, i) for i in devices if i - distance in devices]
    return lax.ppermute(block, axis, route)


def product(first, second, first_dim, second_dim):
    return lax.dot_general(
        first,
        second,
        (((first_dim,), (second_dim,)), ((), ())),
        precision=highest_precision,
        preferred_element_type=jnp.float32,
    )


@jax.custom_vjp
def mul_nn(first, second):
    return product(first, second, 1, 0)


@jax.custom_vjp
def mul_nt(first, second):
    return product(first, second, 1, 1)


@jax.custom_vjp
def mul_tn(first, second):
    return product(first, second, 0, 0)


mul_nn.defvjp(
    lambda a, b: (product(a, b, 1, 0), (a, b)),
    lambda res, ct: (product(ct, res[1], 1, 1), product(res[0], ct, 0, 0)),
)
mul_nt.defvjp(
    lambda a, b: (product(a, b, 1, 1), (a, b)),
    lambda res, ct: (product(ct, res[1], 1, 0), product(ct, res[0], 0, 0)),
)
mul_tn.defvjp(
    lambda a, b: (product(a, b, 0, 0), (a, b)),
    lambda res, ct: (product(res[1], ct, 1, 1), product(res[0], ct, 1, 0)),
)


@jax.custom_vjp
def solve_with(inverse, lower, rhs):
    return product(inverse, rhs, 1, 0)


def solve_forward(inverse, lower, rhs):
    solved = product(inverse, rhs, 1, 0)
    return solved, (inverse, solved)


def solve_backward(res, ct):
    inverse, solved = res
    rhs_grad = product(inverse, ct, 0, 0)
    return jnp.zeros_like(inverse), -product(rhs_grad, solved, 1, 1), rhs_grad


solve_with.defvjp(solve_forward, solve_backward)


def square_masks(size):
    rows = lax.broadcasted_iota(jnp.int32, (size, size), 0)
    cols = lax.broadcasted_iota(jnp.int32, (size, size), 1)
    return rows, cols


def unit_lower_inverse(lower):
    size = lower.shape[0]
    rows, cols = square_masks(size)
    inverse = jnp.where(rows == cols, 1.0, 0.0).astype(jnp.float32)
    level = 0
    while (1 << level) < size:
        width = 1 << level
        joined = (rows // (2 * width)) == (cols // (2 * width))
        mask = joined & ((rows // width) > (cols // width))
        off = jnp.where(mask, lower, 0.0)
        if level == 0:
            inverse = inverse - off
        else:
            inverse = inverse - product(product(inverse, off, 1, 0), inverse, 1, 0)
        level += 1
    return inverse


def silu_rows(x):
    return x * lax.logistic(x)


def unit_rows(matrix):
    return matrix * lax.rsqrt(jnp.sum(matrix * matrix, axis=1, keepdims=True) + epsilon)


def piece_terms(query_in, key_in, value_in, decay, strength, nn, nt):
    size = query_in.shape[0]
    width = query_in.shape[1]
    rows, cols = square_masks(size)
    strict = rows > cols
    inclusive = rows >= cols
    ones_low = jnp.where(inclusive, 1.0, 0.0).astype(jnp.float32)
    ones_high = jnp.where(rows < cols, 1.0, 0.0).astype(jnp.float32)
    queries = unit_rows(silu_rows(query_in)) * (1.0 / math.sqrt(width))
    keys = unit_rows(silu_rows(key_in))
    values = silu_rows(value_in)
    gaps = nn(ones_low, jnp.where(strict, jnp.broadcast_to(decay, (size, size)), 0.0))
    spread = jnp.exp(gaps)
    decay_wide = jnp.broadcast_to(decay, (size, width))
    head_decay = jnp.exp(nn(ones_low, decay_wide))
    tail_decay = jnp.exp(nn(ones_high, decay_wide))
    final = jnp.exp(jnp.sum(decay, axis=0, keepdims=True))
    lower = jnp.where(strict, spread * nt(keys, keys), 0.0) * strength
    scores = jnp.where(inclusive, spread * nt(queries, keys), 0.0)
    return (
        lower,
        scores,
        head_decay * queries,
        head_decay * keys,
        tail_decay * keys,
        values,
        final,
    )


def plain_nn(a, b):
    return product(a, b, 1, 0)


def plain_nt(a, b):
    return product(a, b, 1, 1)


def forward_kernel(q_ref, k_ref, v_ref, d_ref, s_ref, x_ref, o_ref, e_ref, m_ref, f_ref):
    strength = s_ref[...]
    lower, scores, led_queries, led_keys, tail_keys, values, final = piece_terms(
        q_ref[...], k_ref[...], v_ref[...], d_ref[...], strength, plain_nn, plain_nt
    )
    inverse = unit_lower_inverse(lower)
    x_ref[...] = inverse
    direct = product(inverse, strength * values, 1, 0)
    across = product(inverse, strength * led_keys, 1, 0)
    o_ref[...] = product(scores, direct, 1, 0)
    e_ref[...] = led_queries - product(scores, across, 1, 0)
    width = led_keys.shape[1]
    rows, cols = square_masks(width)
    m_ref[...] = jnp.where(rows == cols, jnp.broadcast_to(final, (width, width)), 0.0) - product(
        tail_keys, across, 0, 0
    )
    f_ref[...] = product(tail_keys, direct, 0, 0)


def backward_kernel(
    q_ref, k_ref, v_ref, d_ref, s_ref, x_ref, i_ref, g_ref, t_ref,
    dq_ref, dk_ref, dv_ref, dd_ref, ds_ref,
):
    inverse = x_ref[...]
    start = i_ref[...]

    def run(query_in, key_in, value_in, decay, strength):
        lower, scores, led_queries, led_keys, tail_keys, values, final = piece_terms(
            query_in, key_in, value_in, decay, strength, mul_nn, mul_nt
        )
        update = solve_with(inverse, lower, strength * (values - mul_nn(led_keys, start)))
        mixed = mul_nn(led_queries, start) + mul_nn(scores, update)
        last = final * start + mul_tn(tail_keys, update)
        return mixed, last

    unused, pull = jax.vjp(run, q_ref[...], k_ref[...], v_ref[...], d_ref[...], s_ref[...])
    grads = pull((g_ref[...], t_ref[...]))
    for ref, grad in zip((dq_ref, dk_ref, dv_ref, dd_ref, ds_ref), grads):
        ref[...] = grad


def out_gate(mixer_rows, gate_rows, gain_row):
    scale = lax.rsqrt(jnp.mean(mixer_rows * mixer_rows, axis=1, keepdims=True) + epsilon)
    return mixer_rows * scale * gain_row * silu_rows(gate_rows)


def gate_kernel(o_ref, e_ref, i_ref, gate_ref, gain_ref, out_ref):
    mixer_rows = o_ref[...] + product(e_ref[...], i_ref[...], 1, 0)
    gated = out_gate(mixer_rows, gate_ref[...].astype(jnp.float32), gain_ref[...])
    out_ref[...] = gated.astype(out_ref.dtype)


def gate_back_kernel(
    o_ref, e_ref, i_ref, gate_ref, gain_ref, grad_ref, mg_ref, gg_ref, ng_ref, r_ref
):
    effect = e_ref[...]
    mixer_rows = o_ref[...] + product(effect, i_ref[...], 1, 0)
    unused, pull = jax.vjp(
        out_gate, mixer_rows, gate_ref[...].astype(jnp.float32), gain_ref[...]
    )
    mixer_grad, gate_grad, gain_grad = pull(grad_ref[...].astype(jnp.float32))
    mg_ref[...] = mixer_grad
    gg_ref[...] = gate_grad.astype(gg_ref.dtype)
    ng_ref[...] = gain_grad
    r_ref[...] = product(effect, mixer_grad, 0, 0)


def per_head(kernel, grid, ins, outs, args, flops):
    return pl.pallas_call(
        kernel,
        grid=grid,
        in_specs=ins,
        out_specs=[spec for spec, _ in outs],
        out_shape=[shape for _, shape in outs],
        cost_estimate=pl.CostEstimate(
            flops=flops, bytes_accessed=sum(a.size * a.dtype.itemsize for a in args), transcendentals=0
        ),
    )(*args)


def columns(rows, width, first):
    return pl.BlockSpec((rows, width), lambda h, c, first=first: (c, first + h))


def heads_spec(*shape):
    return pl.BlockSpec((None, None) + shape, lambda h, c: (h, c) + (0,) * len(shape))


def of_shape(shape, kind=jnp.float32):
    return jax.ShapeDtypeStruct(shape, kind)


def state_product(state_map, held):
    return jnp.einsum("hij,hjv->hiv", state_map, held, precision=highest_precision)


def state_pull(state_map, held):
    return jnp.einsum("hji,hjv->hiv", state_map, held, precision=highest_precision)


def mat_nt(first_mat, second_mat):
    return lax.dot_general(
        first_mat, second_mat, (((1,), (1,)), ((), ())), preferred_element_type=jnp.float32
    )


def mat_tn(first_mat, second_mat):
    return lax.dot_general(
        first_mat, second_mat, (((0,), (0,)), ((), ())), preferred_element_type=jnp.float32
    )


def mat_nn(first_mat, second_mat):
    return jnp.dot(first_mat, second_mat, preferred_element_type=jnp.float32)


def rms_scale(hidden, gain_vec):
    return (
        hidden * lax.rsqrt(jnp.mean(hidden * hidden, axis=-1, keepdims=True) + epsilon) * gain_vec
    )


def swiglu(gate_part, up_part):
    return jax.nn.silu(gate_part) * up_part


def short_conv(padded, conv_all):
    length = padded.shape[0] - (KW - 1)
    mixed_rows = padded[0:length] * conv_all[0]
    for tap_index in range(1, KW):
        mixed_rows = mixed_rows + padded[tap_index : tap_index + length] * conv_all[tap_index]
    return mixed_rows


def decay_rates(rates, decay_log, decay_bias):
    heads = decay_log.shape[0]
    pairs = jnp.transpose(rates.reshape(rates.shape[0], heads, 2), (2, 1, 0))
    log_decay = -jnp.exp(decay_log)[:, None] * jax.nn.softplus(pairs[0] + decay_bias[:, None])
    strength = jax.nn.sigmoid(pairs[1])
    return log_decay[:, :, None], strength[:, :, None]


def split_columns(matrix, widths):
    pieces = []
    offset_col = 0
    for width_one in widths:
        pieces.append(matrix[:, offset_col : offset_col + width_one])
        offset_col = offset_col + width_one
    return pieces


def head_halves(weights, parts):
    slabs = []
    for part in range(parts):
        cut = []
        for weight in weights:
            width = weight.shape[1] // parts
            cut.append(weight[:, part * width : (part + 1) * width])
        slabs.append(jnp.concatenate(cut, axis=1))
    return jnp.stack(slabs)


def swap_halves(slabs):
    return lax.all_to_all(slabs, "head", split_axis=0, concat_axis=0, tiled=True)


def whole_rows(slabs):
    full = lax.all_gather(slabs, ("ctx", "batch"), axis=1, tiled=True)
    return full.reshape(full.shape[0] * full.shape[1], full.shape[2])


def other_parts(block):
    parts = lax.axis_size("head")
    total = None
    for shift in range(1, parts):
        moved = lax.ppermute(block, "head", [(i, (i + shift) % parts) for i in range(parts)])
        moved = moved.astype(jnp.float32)
        total = moved if total is None else total + moved
    return total


def head_sum(partial, kind=jnp.bfloat16):
    sent = partial.astype(kind)
    if lax.axis_size("head") == 1:
        return sent.astype(jnp.float32)
    return sent.astype(jnp.float32) + other_parts(sent)


def own_rows_sum(partial):
    parts = lax.axis_size("head")
    rows = partial.shape[0] // parts
    me = lax.axis_index("head")
    total = lax.dynamic_slice_in_dim(partial, me * rows, rows, 0)
    for shift in range(1, parts):
        target = lax.rem(me + shift, parts)
        sent = lax.dynamic_slice_in_dim(partial, target * rows, rows, 0).astype(jnp.bfloat16)
        route = [(i, (i + shift) % parts) for i in range(parts)]
        total = total + lax.ppermute(sent, "head", route).astype(jnp.float32)
    return total


def body(
    tokens,
    cotangent,
    norm1_gain,
    w_query,
    w_key,
    w_value,
    w_gate,
    w_rates,
    conv_query,
    conv_key,
    conv_value,
    decay_log,
    decay_bias,
    out_gain,
    w_out,
    norm2_gain,
    w_ffgate,
    w_ffup,
    w_down,
):
    parts = lax.axis_size("head")
    me = lax.axis_index("head")
    heads = decay_log.shape[0]
    query_width = conv_query.shape[1]
    value_width = conv_value.shape[1]
    dk = query_width // heads
    dv = value_width // heads
    margin = KW - 1
    gains = jnp.stack([norm1_gain, norm2_gain], axis=1)
    slabs_in = head_halves(
        [w_query, w_key, w_value, w_gate, w_rates, jnp.tile(gains, (1, parts))], parts
    )
    in_weight = whole_rows(swap_halves(slabs_in))
    rates_width = w_rates.shape[1] // parts
    mixed_width = 2 * query_width + value_width
    proj_width = mixed_width + value_width + rates_width
    gain_cols = in_weight[:, proj_width:].astype(jnp.float32)
    gain_one = gain_cols[:, 0]
    gain_two = gain_cols[:, 1]
    later = swap_halves(head_halves([w_out, w_ffgate, w_ffup, w_down], parts))
    ff_local = w_down.shape[1] // parts
    out_weight = whole_rows(later[:, :, :value_width])
    ff_weight = whole_rows(later[:, :, value_width : value_width + 2 * ff_local])
    down_weight = whole_rows(later[:, :, value_width + 2 * ff_local :])

    inputs_tok = tokens[0]
    own_count = inputs_tok.shape[0]
    piece_tok = lax.all_gather(inputs_tok, "head", axis=0, tiled=True)
    cot = lax.all_gather(cotangent[0], "head", axis=0, tiled=True)
    residual = piece_tok.astype(jnp.float32)
    piece_rows = residual.shape[0]
    normed_one = rms_scale(residual, gain_one).astype(jnp.bfloat16)
    proj = mat_nn(normed_one, in_weight[:, :proj_width]).astype(jnp.bfloat16)
    joined = proj[:, :mixed_width]
    rates_here = proj[:, mixed_width + value_width :]
    rim_rows = passed_along(joined[piece_rows - margin :], "ctx", 1)
    padded = jnp.concatenate([rim_rows, joined], axis=0).astype(jnp.float32)
    conv_all = jnp.concatenate([conv_query, conv_key, conv_value], axis=1).astype(jnp.float32)
    mixed, conv_vjp = jax.vjp(short_conv, padded, conv_all)
    (log_decay, strength), rates_vjp = jax.vjp(
        decay_rates, rates_here.astype(jnp.float32), decay_log, decay_bias
    )
    value_first = 2 * query_width // dv
    chunk = min(CHUNK, piece_rows)
    chunks = piece_rows // chunk
    grid = (heads, chunks)
    log_decay = log_decay.reshape(heads, chunks, chunk, 1)
    strength = strength.reshape(heads, chunks, chunk, 1)
    mixed_specs = [
        columns(chunk, dk, 0),
        columns(chunk, dk, heads),
        columns(chunk, dv, value_first),
        heads_spec(chunk, 1),
        heads_spec(chunk, 1),
    ]
    square = heads_spec(chunk, chunk)
    state = heads_spec(dk, dv)
    rows_v = columns(chunk, dv, 0)
    rows_k = columns(chunk, dk, 0)
    inverse, local_out, effect, state_map, state_offset = per_head(
        forward_kernel,
        grid,
        mixed_specs,
        [
            (square, of_shape((heads, chunks, chunk, chunk))),
            (rows_v, of_shape((piece_rows, value_width))),
            (rows_k, of_shape((piece_rows, query_width))),
            (heads_spec(dk, dk), of_shape((heads, chunks, dk, dk))),
            (state, of_shape((heads, chunks, dk, dv))),
        ],
        (mixed, mixed, mixed, log_decay, strength),
        heads * 100 * piece_rows * chunk**2,
    )
    chunk_maps = [state_map[:, i] for i in range(chunks)]
    chunk_offsets = [state_offset[:, i] for i in range(chunks)]
    piece_map = chunk_maps[0]
    piece_offset = chunk_offsets[0]
    for i in range(1, chunks):
        piece_map = state_product(chunk_maps[i], piece_map)
        piece_offset = state_product(chunk_maps[i], piece_offset) + chunk_offsets[i]
    last_step = lax.axis_size("ctx") - 1
    start_state = jnp.zeros_like(piece_offset)
    for step in range(last_step):
        moved = piece_offset
        if step > 0:
            moved = moved + state_product(piece_map, start_state)
        start_state = passed_along(moved.astype(jnp.bfloat16), "ctx", 1).astype(jnp.float32)
    starts = [start_state]
    for i in range(1, chunks):
        starts.append(state_product(chunk_maps[i - 1], starts[-1]) + chunk_offsets[i - 1])
    start_states = jnp.stack(starts, axis=1)
    gain_row = out_gain.astype(jnp.float32)[None]
    gate_spec = columns(chunk, dv, mixed_width // dv)
    gain_spec = pl.BlockSpec((1, dv), lambda h, c: (0, h))
    gain_out = pl.BlockSpec((None, 1, dv), lambda h, c: (c, 0, h))
    gate_ins = [rows_v, rows_k, state, gate_spec, gain_spec]
    gate_args = (local_out, effect, start_states, proj, gain_row)
    (gated,) = per_head(
        gate_kernel,
        grid,
        gate_ins,
        [(rows_v, of_shape((piece_rows, value_width), jnp.bfloat16))],
        gate_args,
        heads * 12 * piece_rows * dk * dv,
    )
    middle = residual + head_sum(mat_nt(gated, out_weight))
    normed_two_f, norm_two_vjp = jax.vjp(rms_scale, middle, gain_two)
    normed_two = normed_two_f.astype(jnp.bfloat16)
    ff_both = mat_nn(normed_two, ff_weight)
    hidden_f, swiglu_vjp = jax.vjp(swiglu, ff_both[:, :ff_local], ff_both[:, ff_local:])
    hidden = hidden_f.astype(jnp.bfloat16)
    hidden_grad = mat_nn(cot, down_weight)
    gate_grad_f, up_grad_f = swiglu_vjp(hidden_grad)
    ff_grads = jnp.concatenate([gate_grad_f, up_grad_f], axis=1).astype(jnp.bfloat16)
    middle_part, gain_two_grad = norm_two_vjp(head_sum(mat_nt(ff_grads, ff_weight)))
    middle_grad = cot.astype(jnp.float32) + middle_part
    middle_grad_b = middle_grad.astype(jnp.bfloat16)
    gated_grad = mat_nn(middle_grad_b, out_weight).astype(jnp.bfloat16)
    middle_own = lax.dynamic_slice_in_dim(middle, me * own_count, own_count, 0)
    output_tok = (middle_own + own_rows_sum(mat_nt(hidden, down_weight))).astype(jnp.bfloat16)

    mixer_grad, gate_bf, out_gain_grad, reach = per_head(
        gate_back_kernel,
        grid,
        gate_ins + [rows_v],
        [
            (rows_v, of_shape((piece_rows, value_width))),
            (rows_v, of_shape((piece_rows, value_width), jnp.bfloat16)),
            (gain_out, of_shape((chunks, 1, value_width))),
            (state, of_shape((heads, chunks, dk, dv))),
        ],
        gate_args + (gated_grad,),
        heads * 24 * piece_rows * dk * dv,
    )
    chunk_reach = [reach[:, i] for i in range(chunks)]
    piece_reach = chunk_reach[chunks - 1]
    for i in range(chunks - 2, -1, -1):
        piece_reach = chunk_reach[i] + state_pull(chunk_maps[i], piece_reach)
    last_grad = jnp.zeros_like(piece_reach)
    for step in range(last_step):
        moved = piece_reach
        if step > 0:
            moved = moved + state_pull(piece_map, last_grad)
        last_grad = passed_along(moved.astype(jnp.bfloat16), "ctx", -1).astype(jnp.float32)
    lasts = [last_grad]
    for i in range(chunks - 1, 0, -1):
        lasts.insert(0, chunk_reach[i] + state_pull(chunk_maps[i], lasts[0]))
    last_grads = jnp.stack(lasts, axis=1)

    ff_sums = lax.psum_scatter(
        jnp.concatenate(
            [
                mat_tn(middle_grad_b, gated).astype(jnp.bfloat16),
                mat_tn(normed_two, ff_grads).astype(jnp.bfloat16),
                mat_tn(cot, hidden).astype(jnp.bfloat16),
            ],
            axis=1,
        ),
        ("ctx", "batch"),
        scatter_dimension=0,
        tiled=True,
    ).astype(jnp.float32)
    ff_parts = split_columns(ff_sums, (value_width, ff_local, ff_local, ff_local))

    query_g, key_g, value_g, decay_g, strength_g = per_head(
        backward_kernel,
        grid,
        mixed_specs + [square, state, rows_v, state],
        [
            (rows_k, of_shape((piece_rows, query_width))),
            (rows_k, of_shape((piece_rows, query_width))),
            (rows_v, of_shape((piece_rows, value_width))),
            (heads_spec(chunk, 1), of_shape((heads, chunks, chunk, 1))),
            (heads_spec(chunk, 1), of_shape((heads, chunks, chunk, 1))),
        ],
        (mixed, mixed, mixed, log_decay, strength, inverse, start_states, mixer_grad, last_grads),
        heads * 100 * piece_rows * chunk**2,
    )
    padded_grad, conv_grad = conv_vjp(jnp.concatenate([query_g, key_g, value_g], axis=1))
    rates_grad_f, decay_log_grad, decay_bias_grad = rates_vjp(
        (decay_g.reshape(heads, piece_rows, 1), strength_g.reshape(heads, piece_rows, 1))
    )
    back_rim = passed_along(padded_grad[:margin], "ctx", -1)
    own_rows = padded_grad[margin:]
    own_rows = jnp.concatenate(
        [own_rows[: piece_rows - margin], own_rows[piece_rows - margin :] + back_rim], axis=0
    ).astype(jnp.bfloat16)
    proj_grad = jnp.concatenate([own_rows, gate_bf, rates_grad_f.astype(jnp.bfloat16)], axis=1)
    proj_sums = lax.psum_scatter(
        mat_tn(normed_one, proj_grad).astype(jnp.bfloat16),
        ("ctx", "batch"),
        scatter_dimension=0,
        tiled=True,
    ).astype(jnp.float32)
    proj_parts = split_columns(
        proj_sums, (query_width, query_width, value_width, value_width, rates_width)
    )
    own_grad = own_rows_sum(mat_nt(proj_grad, in_weight[:, :proj_width]))
    unused_rows, norm_one_vjp = jax.vjp(rms_scale, inputs_tok.astype(jnp.float32), gain_one)
    input_part, gain_one_grad = norm_one_vjp(own_grad)
    input_grad = lax.dynamic_slice_in_dim(middle_grad, me * own_count, own_count, 0) + input_part
    smalls = (
        conv_grad.reshape(-1),
        jnp.sum(out_gain_grad, axis=(0, 1)),
        head_sum(gain_one_grad, jnp.float32),
        gain_two_grad,
        decay_log_grad,
        decay_bias_grad,
    )
    summed = lax.psum(jnp.concatenate(smalls), ("ctx", "batch"))
    cuts = []
    first = 0
    for small in smalls:
        cuts.append(summed[first : first + small.shape[0]])
        first += small.shape[0]
    conv_sum = cuts[0].reshape(conv_grad.shape)
    share = norm1_gain.shape[0]
    place = (me * lax.axis_size("ctx") + lax.axis_index("ctx")) * lax.axis_size("batch")
    place = (place + lax.axis_index("batch")) * share
    return (
        output_tok[None],
        input_grad[None],
        lax.dynamic_slice_in_dim(cuts[2], place, share, 0),
        proj_parts[0],
        proj_parts[1],
        proj_parts[2],
        proj_parts[3],
        proj_parts[4],
        conv_sum[:, :query_width],
        conv_sum[:, query_width : 2 * query_width],
        conv_sum[:, 2 * query_width :],
        cuts[4],
        cuts[5],
        cuts[1],
        ff_parts[0],
        lax.dynamic_slice_in_dim(cuts[3], place, share, 0),
        ff_parts[1],
        ff_parts[2],
        ff_parts[3],
    )


def solution(mesh):
    placed = (
        P("batch", ("ctx", "head"), None),
        P("batch", ("ctx", "head"), None),
        P(("head", "ctx", "batch")),
        P(("head", "ctx", "batch"), None),
        P(("head", "ctx", "batch"), None),
        P(("head", "ctx", "batch"), None),
        P(("head", "ctx", "batch"), None),
        P(("head", "ctx", "batch"), None),
        P(None, "head"),
        P(None, "head"),
        P(None, "head"),
        P("head"),
        P("head"),
        P("head"),
        P(("head", "ctx", "batch"), None),
        P(("head", "ctx", "batch")),
        P(("head", "ctx", "batch"), None),
        P(("head", "ctx", "batch"), None),
        P(("head", "ctx", "batch"), None),
    )
    return jax.shard_map(
        body,
        mesh=mesh,
        in_specs=placed,
        out_specs=(
            P("batch", ("ctx", "head"), None),
            P("batch", ("ctx", "head"), None),
            P(("head", "ctx", "batch")),
            P(("ctx", "batch"), "head"),
            P(("ctx", "batch"), "head"),
            P(("ctx", "batch"), "head"),
            P(("ctx", "batch"), "head"),
            P(("ctx", "batch"), "head"),
            P(None, "head"),
            P(None, "head"),
            P(None, "head"),
            P("head"),
            P("head"),
            P("head"),
            P(("ctx", "batch"), "head"),
            P(("head", "ctx", "batch")),
            P(("ctx", "batch"), "head"),
            P(("ctx", "batch"), "head"),
            P(("ctx", "batch"), "head"),
        ),
        check_vma=False,
    )
```
